32 devices in a mesh: ctx: 16 (over z, y, core), fs: 2 (over x).
Axes of the slice: x: 2, y: 2, z: 4, core: 2. Of those that a mesh axis runs over, the one named last changes fastest.
Arguments:
- tokens: float32 [4096, 960], P(('ctx', 'fs')), may hold values from -6 to 6
- positions: int32 [4096], P(('ctx', 'fs')), may hold values from 0 to 4095, as said below
- attn_gain: bfloat16 [960], P('fs'), may hold values from 0.099609375 to 1.8984375
- w_query: bfloat16 [960, 960], P('fs'), may hold values from -21 to 21
- w_kv: bfloat16 [960, 640], P('fs'), may hold values from -1 to 1
- w_out: bfloat16 [960, 960], P('fs'), may hold values from -3.5 to 3.5
- mlp_gain: bfloat16 [960], P('fs'), may hold values from 0.099609375 to 1.8984375
- w_gate: bfloat16 [960, 2560], P('fs'), may hold values from -0.1875 to 0.1875
- w_up: bfloat16 [960, 2560], P('fs'), may hold values from -0.1875 to 0.1875
- w_down: bfloat16 [2560, 960], P('fs'), may hold values from -0.125 to 0.125
- cotangent: float32 [4096, 960], P(('ctx', 'fs')), may hold values from -12 to 12
Outputs:
- result: float32 [4096, 960], P(('ctx', 'fs'))
- grad_tokens: float32 [4096, 960], P(('ctx', 'fs'))
- grad_attn_gain: float32 [960], P('fs')
- grad_query: float32 [960, 960], P('fs')
- grad_kv: float32 [960, 640], P('fs')
- grad_out: float32 [960, 960], P('fs')
- grad_mlp_gain: float32 [960], P('fs')
- grad_gate: float32 [960, 2560], P('fs')
- grad_up: float32 [960, 2560], P('fs')
- grad_down: float32 [2560, 960], P('fs')
The draws below stay inside these ranges and needn't reach their ends.
Inputs may be any that keep to these rules, and one draw needn't show every extreme that they name: `positions`: a permutation of 0 to 4095 in which each aligned run of 128 entries holds consecutive rising values.
All inputs are finite; a program needn't handle non-finite values.
Results may differ from the reference program's by a relative error of at most 0.02.
Values may be sent and summed in bfloat16 or wider, within the bound.
A program may use at most 256 MiB of HBM per device.

```python
import math
import jax
import jax.numpy as jnp
from jax import lax

D = 960
HQ = 15
KVH = 5
HD = 64
FF = 2560
TOK_DEV = 128
SEQ = 4096


def draw_positions(key, part):
    order = jax.random.permutation(key, SEQ // TOK_DEV)
    within = jnp.arange(TOK_DEV, dtype=jnp.int32)
    return (order.astype(jnp.int32)[:, None] * TOK_DEV + within[None, :]).reshape(SEQ).astype(jnp.int32)


def key_columns(key):
    return jax.random.truncated_normal(jax.random.fold_in(key, 11), -4.0, 4.0, (D, KVH * HD), jnp.float32) / math.sqrt(D)


def draw_w_kv(key, part):
    value_columns = jax.random.truncated_normal(jax.random.fold_in(key, 12), -4.0, 4.0, (D, KVH * HD), jnp.float32) / math.sqrt(D)
    return jnp.concatenate([key_columns(key), value_columns], axis=1).astype(jnp.bfloat16)


def draw_w_query(key, part):
    fresh = jax.random.truncated_normal(jax.random.fold_in(key, 13), -4.0, 4.0, (D, HQ * HD), jnp.float32) / math.sqrt(D)
    return fresh.astype(jnp.bfloat16)


def draw_cotangent(key, part):
    rising = jnp.arange(SEQ, dtype=jnp.float32)[:, None] / SEQ
    normal_part = jax.random.truncated_normal(key, -4.0, 4.0, (SEQ, D), jnp.float32)
    return (normal_part * jnp.exp(rising * math.log(3.0))).astype(jnp.float32)


def levels(own_key, extent, shards, low, top_value):
    def one(axis_at, blocks):
        heights = jax.random.uniform(jax.random.fold_in(jax.random.fold_in(own_key, 6), axis_at), (blocks,), jnp.float32, low / len(shards), top_value / len(shards))
        return jnp.repeat(jnp.exp(heights), extent[axis_at] // blocks).reshape((-1,) + (1,) * (len(extent) - axis_at - 1))

    gain = one(*shards[0])
    for cut in shards[1:]:
        gain = gain * one(*cut)
    return gain


def gaussian(own_key, shape, width, most, split=(), kind=jnp.bfloat16):
    loudness = levels(own_key, shape, split, -0.22, 0.18) if split else 1.0
    entries = jax.random.normal(own_key, shape, jnp.float32) * width * loudness
    return jnp.minimum(jnp.maximum(entries, -most), most).astype(kind)


def setup_inputs(seed: int = 0) -> dict:
    seeds = jax.random.split(jax.random.key(seed), 12)
    tokens = gaussian(seeds[0], (SEQ, D), 1.0, 6.0, ((0, 32),), jnp.float32)
    positions = draw_positions(jax.random.fold_in(seeds[11], 71), 0)
    attn_gain = jnp.clip(1.0 + 0.18 * jax.random.normal(seeds[2], (D,), jnp.float32), 0.099609375, 1.8984375).astype(jnp.bfloat16)
    w_query = draw_w_query(jax.random.fold_in(seeds[11], 71), 0)
    w_kv = draw_w_kv(jax.random.fold_in(seeds[11], 71), 0)
    w_out = gaussian(seeds[5], (HQ * HD, D), (max(HQ * HD // 320, 1)) ** -0.5, 3.5, ((0, 2),))
    mlp_gain = jnp.clip(1.0 + 0.18 * jax.random.normal(seeds[6], (D,), jnp.float32), 0.099609375, 1.8984375).astype(jnp.bfloat16)
    w_gate = gaussian(seeds[7], (D, FF), D ** -0.5, 0.1875, ((0, 2),))
    w_up = gaussian(seeds[8], (D, FF), D ** -0.5, 0.1875, ((0, 2),))
    w_down = gaussian(seeds[9], (FF, D), FF ** -0.5, 0.125, ((0, 2),))
    cotangent = draw_cotangent(jax.random.fold_in(seeds[11], 71), 0)
    return dict(tokens=tokens, positions=positions, attn_gain=attn_gain, w_query=w_query, w_kv=w_kv, w_out=w_out, mlp_gain=mlp_gain, w_gate=w_gate, w_up=w_up, w_down=w_down, cotangent=cotangent)


norm_eps = 1e-05
rope_base = 10000.0
neg_large = -1e+30

def rms_scale(hidden_rows):
    return lax.rsqrt(lax.optimization_barrier(jnp.mean(hidden_rows * hidden_rows, axis=-1, keepdims=True)) + norm_eps)

def rope_tables(positions):
    half_width = HD // 2
    frequency = rope_base ** (-(jnp.arange(half_width, dtype=jnp.float32) * (2.0 / HD)))
    angles = positions.astype(jnp.float32)[:, None] * frequency[None, :]
    return (jnp.cos(angles)[:, None, :], jnp.sin(angles)[:, None, :])

def rotate(values, cosine, sine_table):
    half_width = values.shape[-1] // 2
    first_half = values[..., :half_width]
    second_half = values[..., half_width:]
    return jnp.concatenate([first_half * cosine - second_half * sine_table, second_half * cosine + first_half * sine_table], axis=-1)

def norm_back(grad_gained, normed, scale_rows, gain_row):
    grad_normed = grad_gained * gain_row
    grad_gain = lax.optimization_barrier(jnp.sum(grad_gained * normed, axis=0))
    inner_mean = lax.optimization_barrier(jnp.mean(grad_normed * normed, axis=-1, keepdims=True))
    return (scale_rows * (grad_normed - normed * inner_mean), grad_gain)

def reference(tokens, positions, attn_gain, w_query, w_kv, w_out, mlp_gain, w_gate, w_up, w_down, cotangent):
    groups = HQ // KVH
    score_scale = HD ** (-0.5)
    block_rows = 256 if SEQ % 256 == 0 else SEQ
    block_count = SEQ // block_rows
    cosine, sine_table = rope_tables(positions)
    gain_one = attn_gain.astype(jnp.float32)
    gain_two = mlp_gain.astype(jnp.float32)
    scale_one = rms_scale(tokens)
    normed_one = tokens * scale_one
    inputs_one = (normed_one * gain_one).astype(jnp.bfloat16)
    query_linear = jnp.dot(inputs_one, w_query, preferred_element_type=jnp.float32).reshape(SEQ, HQ, HD)
    queries = lax.optimization_barrier(rotate(query_linear, cosine, sine_table).astype(jnp.bfloat16))
    pair_linear = jnp.dot(inputs_one, w_kv, preferred_element_type=jnp.float32)
    keys_low = lax.optimization_barrier(rotate(pair_linear[:, :KVH * HD].reshape(SEQ, KVH, HD), cosine, sine_table).astype(jnp.bfloat16))
    values_low = lax.optimization_barrier(pair_linear[:, KVH * HD:].reshape(SEQ, KVH, HD).astype(jnp.bfloat16))
    keys_wide = keys_low.astype(jnp.float32)
    values_wide = values_low.astype(jnp.float32)
    query_blocks = queries.reshape(block_count, block_rows, KVH, groups, HD)
    position_blocks = positions.reshape(block_count, block_rows)

    def masked_scores(query_block, position_block):
        scores = jnp.einsum('bkgd,skd->kgbs', query_block.astype(jnp.float32), keys_wide) * score_scale
        allowed = positions[None, None, None, :] <= position_block[None, None, :, None]
        return jnp.where(allowed, scores, neg_large)

    def forward_block(block_data):
        query_block, position_block = block_data
        masked = masked_scores(query_block, position_block)
        row_top = lax.optimization_barrier(jnp.max(masked, axis=-1, keepdims=True))
        log_total = row_top + jnp.log(lax.optimization_barrier(jnp.sum(jnp.exp(masked - row_top), axis=-1, keepdims=True)))
        soft_weights = jnp.exp(masked - log_total)
        head_outputs = jnp.einsum('kgbs,skd->bkgd', soft_weights, values_wide, precision=lax.Precision.HIGHEST)
        return (head_outputs, log_total[..., 0])
    head_outputs, log_totals = lax.map(forward_block, (query_blocks, position_blocks))
    attn_rows = head_outputs.reshape(SEQ, HQ * HD)
    attn_low = attn_rows.astype(jnp.bfloat16)
    middle = tokens + jnp.dot(attn_low, w_out, preferred_element_type=jnp.float32)
    scale_two = rms_scale(middle)
    normed_two = middle * scale_two
    inputs_two = (normed_two * gain_two).astype(jnp.bfloat16)
    gate_linear = jnp.dot(inputs_two, w_gate, preferred_element_type=jnp.float32)
    up_linear = jnp.dot(inputs_two, w_up, preferred_element_type=jnp.float32)
    sigmoid_gate = jax.nn.sigmoid(gate_linear)
    activated = gate_linear * sigmoid_gate
    hidden = (activated * up_linear).astype(jnp.bfloat16)
    result = middle + jnp.dot(hidden, w_down, preferred_element_type=jnp.float32)
    grad_low = cotangent.astype(jnp.bfloat16)
    grad_down = jnp.dot(hidden.T, grad_low, preferred_element_type=jnp.float32)
    grad_hidden = jnp.dot(grad_low, w_down.T, preferred_element_type=jnp.float32)
    grad_gate_in = (grad_hidden * up_linear * sigmoid_gate * (1.0 + gate_linear * (1.0 - sigmoid_gate))).astype(jnp.bfloat16)
    grad_up_in = (grad_hidden * activated).astype(jnp.bfloat16)
    grad_gate = jnp.dot(inputs_two.T, grad_gate_in, preferred_element_type=jnp.float32)
    grad_up = jnp.dot(inputs_two.T, grad_up_in, preferred_element_type=jnp.float32)
    grad_inputs_two = jnp.dot(grad_gate_in, w_gate.T, preferred_element_type=jnp.float32) + jnp.dot(grad_up_in, w_up.T, preferred_element_type=jnp.float32)
    grad_norm_two, grad_mlp_gain = norm_back(grad_inputs_two, normed_two, scale_two, gain_two)
    grad_middle = cotangent + grad_norm_two
    grad_middle_low = grad_middle.astype(jnp.bfloat16)
    grad_out = jnp.dot(attn_low.T, grad_middle_low, preferred_element_type=jnp.float32)
    grad_attn = lax.optimization_barrier(jnp.dot(grad_middle_low, w_out.T, preferred_element_type=jnp.float32).astype(jnp.bfloat16))
    delta_rows = lax.optimization_barrier(jnp.sum(grad_attn.astype(jnp.float32).reshape(SEQ, HQ, HD) * attn_rows.reshape(SEQ, HQ, HD), axis=-1))
    delta_blocks = jnp.transpose(delta_rows.reshape(block_count, block_rows, KVH, groups), (0, 2, 3, 1))
    dout_blocks = grad_attn.reshape(block_count, block_rows, KVH, groups, HD)

    def backward_block(carried, block_data):
        grad_keys, grad_values = carried
        query_block, position_block, log_block, dout_block, delta_block = block_data
        masked = masked_scores(query_block, position_block)
        soft_weights = jnp.exp(masked - log_block[..., None])
        dout_wide = dout_block.astype(jnp.float32)
        grad_soft = jnp.einsum('bkgd,skd->kgbs', dout_wide, values_wide)
        grad_scores = lax.optimization_barrier((soft_weights * (grad_soft - delta_block[..., None]) * score_scale).astype(jnp.bfloat16)).astype(jnp.float32)
        rounded = lax.optimization_barrier(soft_weights.astype(jnp.bfloat16)).astype(jnp.float32)
        grad_query_block = jnp.einsum('kgbs,skd->bkgd', grad_scores, keys_wide)
        grad_keys = grad_keys + jnp.einsum('kgbs,bkgd->skd', grad_scores, query_block.astype(jnp.float32))
        grad_values = grad_values + jnp.einsum('kgbs,bkgd->skd', rounded, dout_wide)
        return ((grad_keys, grad_values), grad_query_block)
    zero_grads = jnp.zeros((SEQ, KVH, HD), jnp.float32)
    (grad_keys, grad_values), grad_query_rows = lax.scan(backward_block, (zero_grads, zero_grads), (query_blocks, position_blocks, log_totals, dout_blocks, delta_blocks))
    query_back = rotate(grad_query_rows.reshape(SEQ, HQ, HD), cosine, -sine_table).astype(jnp.bfloat16).reshape(SEQ, HQ * HD)
    key_back = rotate(grad_keys, cosine, -sine_table).reshape(SEQ, KVH * HD)
    pair_back = jnp.concatenate([key_back, grad_values.reshape(SEQ, KVH * HD)], axis=1).astype(jnp.bfloat16)
    grad_query = jnp.dot(inputs_one.T, query_back, preferred_element_type=jnp.float32)
    grad_kv = jnp.dot(inputs_one.T, pair_back, preferred_element_type=jnp.float32)
    grad_inputs_one = jnp.dot(query_back, w_query.T, preferred_element_type=jnp.float32) + jnp.dot(pair_back, w_kv.T, preferred_element_type=jnp.float32)
    grad_norm_one, grad_attn_gain = norm_back(grad_inputs_one, normed_one, scale_one, gain_one)
    grad_tokens = grad_middle + grad_norm_one
    return (result, grad_tokens, grad_attn_gain, grad_query, grad_kv, grad_out, grad_mlp_gain, grad_gate, grad_up, grad_down)
```

```python
import functools

import jax
import jax.numpy as jnp
from jax import lax
from jax.experimental import pallas as pl
from jax.experimental.pallas import tpu as pltpu
from jax.sharding import PartitionSpec as P

HQ = 15
KVH = 5
HD = 64


norm_eps = 1e-05
rope_base = 10000.0
neg_large = -1e30
AXES = ("chip", "core", "fs")
CTX = ("chip", "core")
SWAP = [(0, 1), (1, 0)]


def rms_scale(hidden_rows):
    return lax.rsqrt(jnp.mean(hidden_rows * hidden_rows, axis=-1, keepdims=True) + norm_eps)


def rope_tables(positions):
    half_width = HD // 2
    frequency = rope_base ** (-(jnp.arange(half_width, dtype=jnp.float32) * (2.0 / HD)))
    angles = positions.astype(jnp.float32)[:, None] * frequency[None, :]
    return (jnp.cos(angles)[:, None, :], jnp.sin(angles)[:, None, :])


def rotate(values, cosine, sine_table):
    half_width = values.shape[-1] // 2
    first_half = values[..., :half_width]
    second_half = values[..., half_width:]
    return jnp.concatenate(
        [
            first_half * cosine - second_half * sine_table,
            second_half * cosine + first_half * sine_table,
        ],
        axis=-1,
    )


def norm_back(grad_gained, normed, scale_rows, gain_row):
    grad_normed = grad_gained * gain_row
    grad_gain = jnp.sum(grad_gained * normed, axis=0)
    inner_mean = jnp.mean(grad_normed * normed, axis=-1, keepdims=True)
    return (scale_rows * (grad_normed - normed * inner_mean), grad_gain)


TILE = 128


def chunk_of(blocks):
    for size in (4, 2):
        if blocks % size == 0:
            return size
    return 1


def load_chunk(pairs_ref, slots_ref, first, chunk, lane):
    parts = []
    for step in range(chunk):
        row = pl.multiple_of(slots_ref[first + step] * TILE, TILE)
        parts.append(pairs_ref[pl.ds(row, TILE), lane * 128 : (lane + 1) * 128])
    return parts[0] if chunk == 1 else jnp.concatenate(parts, axis=0)


def allowed_mask(first, chunk, block, width):
    rows = lax.broadcasted_iota(jnp.int32, (chunk * TILE, width), 0) + first * TILE
    columns = lax.broadcasted_iota(jnp.int32, (chunk * TILE, width), 1) % TILE + block * TILE
    return rows <= columns


NT = (((1,), (1,)), ((), ()))


def forward_kernel(chunk, slots_ref, own_ref, query_ref, pairs_ref, out_ref, log_ref, top_ref, total_ref):
    block = own_ref[0]
    width = query_ref.shape[1]
    out_ref[...] = jnp.zeros_like(out_ref)
    top_ref[...] = jnp.full_like(top_ref, neg_large)
    total_ref[...] = jnp.zeros_like(total_ref)
    score_scale = HD ** (-0.5)

    def visit(index, masked):
        first = index * chunk
        loaded = [load_chunk(pairs_ref, slots_ref, first, chunk, lane) for lane in range(KVH)]
        flipped = {lane: loaded[lane].T for lane in range(KVH // 2, KVH)}
        if masked:
            allowed = allowed_mask(first, chunk, block, width)
        for head in range(KVH):
            scores = score_scale * lax.dot_general(
                loaded[head // 2], query_ref[head], NT, preferred_element_type=jnp.float32
            )
            if masked:
                scores = jnp.where(allowed, scores, neg_large)
            top = top_ref[head]
            new_top = jnp.maximum(top, jnp.max(scores, axis=0, keepdims=True))
            weights = jnp.exp(scores - new_top)
            factor = jnp.exp(top - new_top)
            top_ref[head] = new_top
            total_ref[head] = total_ref[head] * factor + jnp.sum(weights, axis=0, keepdims=True)
            high = weights.astype(jnp.bfloat16)
            low = (weights - high.astype(jnp.float32)).astype(jnp.bfloat16)
            values = flipped[(KVH + head) // 2]
            out_ref[head] = (
                out_ref[head] * factor
                + jnp.dot(values, high, preferred_element_type=jnp.float32)
                + jnp.dot(values, low, preferred_element_type=jnp.float32)
            )

    whole = block // chunk
    lax.fori_loop(0, whole, lambda i, c: (visit(i, False), c)[1], 0)
    visit(whole, True)
    for head in range(KVH):
        total = total_ref[head]
        out_ref[head] = out_ref[head] / total
        log_ref[head] = top_ref[head] + jnp.log(total)


def backward_kernel(
    chunk, slots_ref, own_ref, query_ref, dout_ref, log_ref, delta_ref, pairs_ref, grad_ref, terms_ref
):
    block = own_ref[0]
    width = query_ref.shape[1]
    grad_ref[...] = jnp.zeros_like(grad_ref)
    score_scale = HD ** (-0.5)
    rows = chunk * TILE

    def visit(index, masked):
        first = index * chunk
        loaded = [load_chunk(pairs_ref, slots_ref, first, chunk, lane) for lane in range(KVH)]
        flipped = {lane: loaded[lane].T for lane in range((KVH + 1) // 2)}
        if masked:
            allowed = allowed_mask(first, chunk, block, width)
        sums = [None] * KVH

        def add(lane, term):
            sums[lane] = term if sums[lane] is None else sums[lane] + term

        for head in range(KVH):
            key_lane, value_lane = head // 2, (KVH + head) // 2
            scores = score_scale * lax.dot_general(
                loaded[key_lane], query_ref[head], NT, preferred_element_type=jnp.float32
            )
            if masked:
                scores = jnp.where(allowed, scores, neg_large)
            weights = jnp.exp(scores - log_ref[head])
            grad_soft = lax.dot_general(
                loaded[value_lane], dout_ref[head], NT, preferred_element_type=jnp.float32
            )
            grad_scores = (weights * (grad_soft - delta_ref[head]) * score_scale).astype(
                jnp.bfloat16
            )
            grad_ref[head] += jnp.dot(
                flipped[key_lane], grad_scores, preferred_element_type=jnp.float32
            )
            add(
                key_lane,
                jnp.dot(grad_scores, query_ref[head], preferred_element_type=jnp.float32),
            )
            add(
                value_lane,
                jnp.dot(
                    weights.astype(jnp.bfloat16),
                    dout_ref[head],
                    preferred_element_type=jnp.float32,
                ),
            )
        for lane in range(KVH):
            for step in range(chunk):
                row = pl.multiple_of(slots_ref[first + step] * TILE, TILE)
                terms_ref[pl.ds(row, TILE), lane * 128 : (lane + 1) * 128] = sums[lane][
                    step * TILE : (step + 1) * TILE
                ].astype(terms_ref.dtype)

    whole = block // chunk
    lax.fori_loop(0, whole, lambda i, c: (visit(i, False), c)[1], 0)
    visit(whole, True)

    def clear(index, carry):
        row = pl.multiple_of(slots_ref[index] * TILE, TILE)
        terms_ref[pl.ds(row, TILE), :] = jnp.zeros((TILE, terms_ref.shape[1]), terms_ref.dtype)
        return carry

    lax.fori_loop((whole + 1) * chunk, slots_ref.shape[0], clear, 0)


def attend(query_pad, pairs, slots, own):
    heads, width, lanes = query_pad.shape
    length = pairs.shape[0]
    smem = pl.BlockSpec(memory_space=pltpu.SMEM)
    vmem = pl.BlockSpec(memory_space=pltpu.VMEM)
    return pl.pallas_call(
        functools.partial(forward_kernel, chunk_of(length // TILE)),
        out_shape=(
            jax.ShapeDtypeStruct((heads, lanes, width), jnp.float32),
            jax.ShapeDtypeStruct((heads, 1, width), jnp.float32),
        ),
        in_specs=[smem, smem, vmem, vmem],
        out_specs=(vmem, vmem),
        scratch_shapes=[
            pltpu.VMEM((heads, 1, width), jnp.float32),
            pltpu.VMEM((heads, 1, width), jnp.float32),
        ],
        compiler_params=pltpu.CompilerParams(vmem_limit_bytes=56 * 2**20),
        cost_estimate=pl.CostEstimate(
            flops=6 * heads * width * length * lanes,
            bytes_accessed=2 * pairs.size,
            transcendentals=heads * width * length,
        ),
        name="attend",
    )(slots, own, query_pad, pairs)


def attend_back(query_pad, dout_pad, logs, deltas, pairs, slots, own):
    heads, width, lanes = query_pad.shape
    length = pairs.shape[0]
    smem = pl.BlockSpec(memory_space=pltpu.SMEM)
    vmem = pl.BlockSpec(memory_space=pltpu.VMEM)
    return pl.pallas_call(
        functools.partial(backward_kernel, chunk_of(length // TILE)),
        out_shape=(
            jax.ShapeDtypeStruct((heads, lanes, width), jnp.float32),
            jax.ShapeDtypeStruct(pairs.shape, jnp.bfloat16),
        ),
        in_specs=[smem, smem, vmem, vmem, vmem, vmem, vmem],
        out_specs=(vmem, vmem),
        compiler_params=pltpu.CompilerParams(vmem_limit_bytes=56 * 2**20),
        cost_estimate=pl.CostEstimate(
            flops=10 * heads * width * length * lanes,
            bytes_accessed=4 * pairs.size,
            transcendentals=heads * width * length,
        ),
        name="attend_back",
    )(slots, own, query_pad, dout_pad, logs, deltas, pairs)


def pad_heads(rows, first_half):
    count = rows.shape[0]
    groups = HQ // KVH
    heads = jnp.transpose(rows.reshape(count, KVH, groups, HD), (1, 2, 0, 3)).reshape(
        KVH, groups * count, HD
    )
    empty = jnp.zeros_like(heads)
    odd = ((jnp.arange(KVH) + first_half) % 2 == 1)[:, None, None]
    return jnp.concatenate([jnp.where(odd, empty, heads), jnp.where(odd, heads, empty)], axis=2)


def unpad_heads(padded, first_half):
    groups = HQ // KVH
    count = padded.shape[2] // groups
    odd = ((jnp.arange(KVH) + first_half) % 2 == 1)[:, None, None]
    heads = jnp.where(odd, padded[:, HD:], padded[:, :HD])
    return jnp.transpose(heads.reshape(KVH, HD, groups, count), (3, 0, 2, 1)).reshape(
        count, HQ * HD
    )


def spread_weight(part):
    cores = lax.axis_size("core")
    rows = part.shape[0] // cores
    own = lax.dynamic_slice_in_dim(part, lax.axis_index("core") * rows, rows, axis=0)
    return lax.all_gather(own, ("fs", "core"), axis=0, tiled=True)


def swap_whole(rows):
    return jnp.concatenate([rows, lax.ppermute(rows, "fs", SWAP)], axis=0)


def swap_tokens(rows, unit):
    half = rows.shape[1] // 2
    unit = unit * lax.axis_size(CTX)
    extra = -half % unit
    first, second = (
        jnp.pad(piece, ((0, 0), (0, extra))) for piece in (rows[:, :half], rows[:, half:])
    )
    lower = lax.axis_index("fs") == 0
    mine, theirs = jnp.where(lower, first, second), jnp.where(lower, second, first)
    return jnp.concatenate([mine, lax.ppermute(theirs, "fs", SWAP)], axis=0)


def ctx_scatter(left, right):
    partial = jnp.dot(left.T, right, preferred_element_type=jnp.float32).astype(jnp.bfloat16)
    return lax.psum_scatter(partial, CTX, scatter_dimension=0, tiled=True)


def ctx_gather(piece, rows):
    return lax.all_gather(piece, CTX, axis=0, tiled=True)[:rows].astype(jnp.float32)


def shards(
    tokens, positions, attn_gain, w_query, w_kv, w_out, mlp_gain, w_gate, w_up, w_down, cotangent
):
    row_count = tokens.shape[0]
    groups = HQ // KVH
    query_width = HQ * HD
    key_width = KVH * HD
    gain_one, gain_two = (
        lax.all_gather(attn_gain, "fs", axis=0, tiled=True),
        lax.all_gather(mlp_gain, "fs", axis=0, tiled=True),
    )
    query_full, pair_full, output_full, gate_full, upward_full, down_full = (
        spread_weight(w_query),
        spread_weight(w_kv),
        spread_weight(w_out),
        spread_weight(w_gate),
        spread_weight(w_up),
        spread_weight(w_down),
    )
    gain_one = gain_one.astype(jnp.float32)
    gain_two = gain_two.astype(jnp.float32)
    cosine, sine_table = rope_tables(positions)
    scale_one = rms_scale(tokens)
    normed_one = tokens * scale_one
    inputs_one = (normed_one * gain_one).astype(jnp.bfloat16)
    query_linear = jnp.dot(inputs_one, query_full, preferred_element_type=jnp.float32).reshape(
        row_count, HQ, HD
    )
    queries = (
        rotate(query_linear, cosine, sine_table)
        .astype(jnp.bfloat16)
        .reshape(row_count, query_width)
    )
    pair_linear = jnp.dot(inputs_one, pair_full, preferred_element_type=jnp.float32)
    keys_rotated = rotate(
        pair_linear[:, :key_width].reshape(row_count, KVH, HD), cosine, sine_table
    ).reshape(row_count, key_width)
    key_values = jnp.concatenate([keys_rotated, pair_linear[:, key_width:]], axis=1).astype(
        jnp.bfloat16
    )
    all_pairs = lax.all_gather(key_values, AXES, axis=0, tiled=True)
    starts = lax.all_gather(positions[:1] // TILE, AXES, axis=0, tiled=True)
    slots = jnp.zeros_like(starts).at[starts].set(jnp.arange(starts.shape[0], dtype=jnp.int32))
    own = positions[:1] // TILE
    query_pad = pad_heads(queries, 0)
    out_pad, logs = attend(query_pad, all_pairs, slots, own)
    attn_rows = unpad_heads(out_pad, KVH)
    attn_low = attn_rows.astype(jnp.bfloat16)
    middle = tokens + jnp.dot(attn_low, output_full, preferred_element_type=jnp.float32)
    scale_two = rms_scale(middle)
    normed_two = middle * scale_two
    inputs_two = (normed_two * gain_two).astype(jnp.bfloat16)
    gate_linear = jnp.dot(inputs_two, gate_full, preferred_element_type=jnp.float32)
    up_linear = jnp.dot(inputs_two, upward_full, preferred_element_type=jnp.float32)
    sigmoid_gate = jax.nn.sigmoid(gate_linear)
    activated = gate_linear * sigmoid_gate
    hidden = (activated * up_linear).astype(jnp.bfloat16)
    result = middle + jnp.dot(hidden, down_full, preferred_element_type=jnp.float32)
    grad_low = cotangent.astype(jnp.bfloat16)
    hidden_both, low_both = swap_tokens(hidden, 1), swap_whole(grad_low)
    down_sum = ctx_scatter(hidden_both, low_both)
    grad_hidden = jnp.dot(grad_low, down_full.T, preferred_element_type=jnp.float32)
    grad_gate_in = (
        grad_hidden * up_linear * sigmoid_gate * (1.0 + gate_linear * (1.0 - sigmoid_gate))
    ).astype(jnp.bfloat16)
    grad_up_in = (grad_hidden * activated).astype(jnp.bfloat16)
    inputs_two_both = swap_tokens(inputs_two, 8)
    gate_up_both = swap_whole(jnp.concatenate([grad_gate_in, grad_up_in], axis=1))
    gate_up_sum = ctx_scatter(inputs_two_both, gate_up_both)
    grad_inputs_two = jnp.dot(
        grad_gate_in, gate_full.T, preferred_element_type=jnp.float32
    ) + jnp.dot(grad_up_in, upward_full.T, preferred_element_type=jnp.float32)
    grad_norm_two, grad_mlp_gain = norm_back(grad_inputs_two, normed_two, scale_two, gain_two)
    grad_middle = cotangent + grad_norm_two
    grad_middle_low = grad_middle.astype(jnp.bfloat16)
    output_sum = ctx_scatter(swap_tokens(attn_low, 8), swap_whole(grad_middle_low))
    grad_attn = jnp.dot(grad_middle_low, output_full.T, preferred_element_type=jnp.float32).astype(
        jnp.bfloat16
    )
    delta_rows = jnp.sum(
        grad_attn.astype(jnp.float32).reshape(row_count, HQ, HD)
        * attn_rows.reshape(row_count, HQ, HD),
        axis=-1,
    )
    deltas = jnp.transpose(delta_rows.reshape(row_count, KVH, groups), (1, 2, 0)).reshape(
        KVH, 1, groups * row_count
    )
    dout_pad = pad_heads(grad_attn, KVH)
    grad_query_pad, term_rows = attend_back(
        query_pad, dout_pad, logs, deltas, all_pairs, slots, own
    )
    summed = lax.psum_scatter(term_rows, AXES, scatter_dimension=0, tiled=True).astype(jnp.float32)
    grad_keys = summed[:, :key_width].reshape(row_count, KVH, HD)
    grad_values = summed[:, key_width:].reshape(row_count, KVH, HD)
    grad_query_rows = unpad_heads(grad_query_pad, 0).reshape(row_count, HQ, HD)
    query_back = (
        rotate(grad_query_rows, cosine, -sine_table)
        .astype(jnp.bfloat16)
        .reshape(row_count, query_width)
    )
    key_back = rotate(grad_keys, cosine, -sine_table).reshape(row_count, key_width)
    pair_back = jnp.concatenate(
        [key_back, grad_values.reshape(row_count, key_width)], axis=1
    ).astype(jnp.bfloat16)
    back_sum = ctx_scatter(
        swap_tokens(inputs_one, 8),
        swap_whole(jnp.concatenate([query_back, pair_back], axis=1)),
    )
    grad_inputs_one = jnp.dot(
        query_back, query_full.T, preferred_element_type=jnp.float32
    ) + jnp.dot(pair_back, pair_full.T, preferred_element_type=jnp.float32)
    grad_norm_one, grad_attn_gain = norm_back(grad_inputs_one, normed_one, scale_one, gain_one)
    grad_tokens = grad_middle + grad_norm_one
    gains = lax.psum(jnp.stack([grad_attn_gain, grad_mlp_gain]), AXES)
    half_width = attn_gain.shape[0]
    gain_grads = lax.dynamic_slice(
        gains, (0, lax.axis_index("fs") * half_width), (2, half_width)
    )
    gate_up = ctx_gather(gate_up_sum, half_width)
    hidden_width = w_gate.shape[1]
    back = ctx_gather(back_sum, half_width)
    return (
        result,
        grad_tokens,
        gain_grads[0],
        back[:, :query_width],
        back[:, query_width:],
        ctx_gather(output_sum, w_out.shape[0]),
        gain_grads[1],
        gate_up[:, :hidden_width],
        gate_up[:, hidden_width:],
        ctx_gather(down_sum, w_down.shape[0]),
    )


def solution(mesh):
    parts, halves = mesh.shape["ctx"], mesh.shape["fs"]
    cores = 2 if parts % 2 == 0 else 1
    fine = jax.sharding.Mesh(mesh.devices.reshape(parts // cores, cores, halves), AXES)
    in_specs = (
        P(AXES, None),
        P(AXES),
        P("fs"),
        P("fs", None),
        P("fs", None),
        P("fs", None),
        P("fs"),
        P("fs", None),
        P("fs", None),
        P("fs", None),
        P(AXES, None),
    )
    out_specs = (
        P(AXES, None),
        P(AXES, None),
        P("fs"),
        P("fs", None),
        P("fs", None),
        P("fs", None),
        P("fs"),
        P("fs", None),
        P("fs", None),
        P("fs", None),
    )
    return jax.shard_map(shards, mesh=fine, in_specs=in_specs, out_specs=out_specs, check_vma=False)
```
